32 devices in a mesh: spin: 2 (over core), band: 16 (over z, y, x).
Axes of the slice: x: 2, y: 2, z: 4, core: 2. Of those that a mesh axis runs over, the one named last changes fastest.
Arguments:
- orbitals: float32 [2, 16, 32768], P('spin', 'band'), may hold values from -15 to 15
- potential: float32 [32768], replicated, may hold values from -6 to 6
Outputs:
- updated: float32 [2, 16, 32768], P('spin', 'band')
- residual: float32 [2, 16, 32768], P('spin', 'band')
The draws below stay inside these ranges and needn't reach their ends.
All inputs are finite; a program needn't handle non-finite values.
Results may differ from the reference program's by a relative error of at most 0.0003.
Values sent between devices are 32-bit elements; how exact they have to be, the bound alone decides.
A program may use at most 128 MiB of HBM per device.

```python
import math
import jax
import jax.numpy as jnp
from jax import lax

SPINS = 2
GRID = 32
G = 32768
BAND_DEV = 1
NB = 16


def draw_orbitals(key, part):
    sample_key, band_key, cell_key = jax.random.split(key, 3)
    band_scale = jnp.exp(jax.random.uniform(band_key, (SPINS, NB, 1), jnp.float32, math.log(0.7), math.log(1.4)))
    planes = (jnp.arange(G, dtype=jnp.int32) // (GRID * GRID)).astype(jnp.float32)
    cell_scale = 0.6 * jnp.exp(planes * (math.log(3.0) / GRID) + jax.random.uniform(cell_key, (G,), jnp.float32, -0.15, 0.15))
    samples = jnp.clip(jax.random.normal(sample_key, (SPINS, NB, G), jnp.float32), -5.0, 5.0)
    return samples * band_scale * cell_scale


def scatter_about(own_key, dims, spread, reach, kind=jnp.bfloat16):
    return jnp.clip(spread * jax.random.normal(own_key, dims, jnp.float32), -reach, reach).astype(kind)


def setup_inputs(seed: int = 0) -> dict:
    keys = jax.random.split(jax.random.key(seed), 3)
    return {
        "orbitals": draw_orbitals(jax.random.fold_in(keys[2], 71), 0),
        "potential": scatter_about(keys[1], (G,), 1.0, 6.0, jnp.float32),
    }


screen_square = 0.04
hartree_weight = 0.03125
mixing = 0.25
step_length = 0.1


def cas_table(points):
    indices = jnp.arange(points, dtype=jnp.int32)
    phase_index = (indices[:, None] * indices[None, :]) % points
    angles = phase_index.astype(jnp.float32) * (2.0 * math.pi / points)
    return jnp.cos(angles) + jnp.sin(angles)


def wave_squares(points):
    indices = jnp.arange(points, dtype=jnp.int32)
    folded = jnp.where(indices < points // 2, indices, indices - points).astype(jnp.float32)
    wavenumber = folded * (math.pi / points)
    squares = wavenumber * wavenumber
    summed = squares[:, None, None] + squares[None, :, None] + squares[None, None, :]
    return summed.reshape(-1)


def hartley(signal, table):
    points = table.shape[0]
    leading = signal.shape[:-1]
    cube_field = signal.reshape((-1, points, points, points))
    for axis_turn in range(3):
        cube_field = jnp.einsum("ka,sabc->sbck", table, cube_field, precision=lax.Precision.HIGHEST)
    return cube_field.reshape(leading + (points ** 3,))


def screened(signal, table, kernel):
    return hartley(kernel * hartley(signal, table), table) / kernel.shape[0]


def reference(orbitals, potential):
    table = cas_table(GRID)
    wave_square = wave_squares(GRID)
    kernel = jnp.where(wave_square > 0, 1.0 / (wave_square + screen_square), 0.0)
    volume = orbitals.shape[2]
    density = jnp.sum(orbitals * orbitals, axis=(0, 1))
    local_field = potential + hartree_weight * screened(density, table, kernel)
    blocks = NB // BAND_DEV
    grouped = orbitals.reshape(SPINS, blocks, BAND_DEV, volume)

    def exchange_block(flat_index):
        spin_index = flat_index // blocks
        block_index = flat_index % blocks
        resident = grouped[spin_index, block_index]
        accumulated = jnp.zeros((BAND_DEV, volume), jnp.float32)
        for offset in (-2, -1, 0, 1, 2):
            partner = grouped[spin_index, (block_index + offset) % blocks]
            pair_field = (resident[:, None, :] * partner[None, :, :]).reshape(-1, volume)
            fields = screened(pair_field, table, kernel).reshape(BAND_DEV, BAND_DEV, volume)
            accumulated = accumulated - jnp.sum(fields * partner[None, :, :], axis=1)
        return accumulated

    exchange_term = lax.map(exchange_block, jnp.arange(SPINS * blocks, dtype=jnp.int32))
    exchange_term = exchange_term.reshape(SPINS, NB, volume)
    kinetic = hartley(0.5 * wave_square * hartley(orbitals, table), table) / volume
    gradient = kinetic + local_field * orbitals + mixing * exchange_term
    first_correlation = jnp.einsum("sjr,sir->sji", orbitals, gradient, precision=lax.Precision.HIGHEST) / volume
    projected = gradient - jnp.einsum("sji,sjr->sir", first_correlation, orbitals, precision=lax.Precision.HIGHEST)
    second_correlation = jnp.einsum("sjr,sir->sji", orbitals, projected, precision=lax.Precision.HIGHEST) / volume
    residual = projected - jnp.einsum("sji,sjr->sir", second_correlation, orbitals, precision=lax.Precision.HIGHEST)
    return orbitals - step_length * residual, residual
```

```python
import functools
import math

import jax
import jax.numpy as jnp
import numpy as np
from jax import lax
from jax.experimental import pallas as pl
from jax.experimental.pallas import tpu as pltpu
from jax.sharding import PartitionSpec as P

screen_square = 0.04
hartree_weight = 0.03125
mixing = 0.25
step_length = 0.1

MESH = pl.DeviceIdType.MESH
LANES = 128


def line_sizes(count):
    power = int(math.log2(count)) if count > 1 else 0
    if 2**power != count:
        return (count, 1, 1)
    fast = 2 ** (power // 3)
    return (count // (fast * fast), fast, fast)


def offsets_of(size):
    if size == 1:
        return (0,)
    if size == 2:
        return (0, 1)
    return tuple(range(-(size - 1), size))


def bf16_split(x):
    high = x.astype(jnp.bfloat16)
    return high, (x - high.astype(jnp.float32)).astype(jnp.bfloat16)


def dot(a, b):
    return jnp.dot(a, b, preferred_element_type=jnp.float32)


class Gather:
    def __init__(self, count, sizes, own, slots, send_sem, recv_sem):
        self.count, self.sizes, self.own, self.slots = count, sizes, own, slots
        self.send_sem, self.recv_sem = send_sem, recv_sem
        self.rows = own.shape[0] // 2
        self.me = lax.axis_index("band")
        self.spin = lax.axis_index("spin")
        strides = (sizes[1] * sizes[2], sizes[2], 1)
        self.strides = strides
        self.coords = tuple(lax.rem(self.me // strides[d], sizes[d]) for d in range(3))
        self.sent = []

    def neighbours(self):
        found = []
        for d in range(3):
            for way in self.ways(d):
                found.append(self.neighbour(d, way))
        return found

    def ways(self, d):
        return () if self.sizes[d] == 1 else (1,) if self.sizes[d] == 2 else (1, -1)

    def neighbour(self, d, way):
        c = self.coords[d]
        if self.sizes[d] == 2:
            return None, self.me + (1 - 2 * c) * self.strides[d]
        guard = c + way < self.sizes[d] if way > 0 else c + way >= 0
        return guard, self.me + way * self.strides[d]

    def part(self, half):
        return pl.ds(half * self.rows, self.rows)

    def send(self, half, block, d, way, guard, mine):
        ok, target = self.neighbour(d, way)
        for extra in (guard,):
            if extra is not None:
                ok = extra if ok is None else jnp.logical_and(ok, extra)
        source = self.own.at[self.part(half)] if mine else self.slots.at[block, self.part(half)]
        copy = pltpu.make_async_remote_copy(
            src_ref=source,
            dst_ref=self.slots.at[block, self.part(half)],
            send_sem=self.send_sem.at[len(self.sent)],
            recv_sem=self.recv_sem.at[half, block],
            device_id=(self.spin, target),
            device_id_type=MESH,
        )
        self.sent.append((ok, copy))
        if ok is None:
            copy.start()
        else:
            pl.when(ok)(copy.start)

    def order(self, half):
        return (0, 1, 2) if half == 0 else (0, 2, 1)

    def send_own(self):
        for half in range(2):
            for d in self.order(half):
                for way in self.ways(d):
                    self.send(half, self.me, d, way, None, True)

    def events(self):
        found = []
        for half in range(2):
            for z in offsets_of(self.sizes[0]):
                for y in offsets_of(self.sizes[1]):
                    for x in offsets_of(self.sizes[2]):
                        if (z, y, x) != (0, 0, 0):
                            found.append((abs(z) + abs(y) + abs(x), half, (z, y, x)))
        return sorted(found, key=lambda e: (e[0], -abs(e[2][0]), e[1]))

    def take(self, half, offsets):
        guard, block = None, self.me
        for d, o in enumerate(offsets):
            if o == 0:
                continue
            c = self.coords[d]
            if self.sizes[d] == 2:
                block = block + (1 - 2 * c) * self.strides[d]
            else:
                ok = c + o < self.sizes[d] if o > 0 else c + o >= 0
                guard = ok if guard is None else jnp.logical_and(guard, ok)
                block = block + o * self.strides[d]
        if guard is not None:
            block = jnp.where(guard, block, self.me)
        arrived = self.slots.at[block, self.part(half)]
        wait = pltpu.make_async_remote_copy(
            src_ref=arrived,
            dst_ref=arrived,
            send_sem=self.send_sem.at[0],
            recv_sem=self.recv_sem.at[half, block],
            device_id=(self.spin, self.me),
            device_id_type=MESH,
        ).wait_recv
        if guard is None:
            wait()
        else:
            pl.when(guard)(wait)
        order = self.order(half)
        last = max(p for p in range(3) if offsets[order[p]] != 0)
        d = order[last]
        if self.sizes[d] > 2:
            self.send(half, block, d, -1 if offsets[d] > 0 else 1, guard, False)
        for later in order[last + 1 :]:
            for way in self.ways(later):
                self.send(half, block, later, way, guard, False)

    def finish(self):
        for ok, copy in self.sent:
            if ok is None:
                copy.wait_send()
            else:
                pl.when(ok)(copy.wait_send)


class DirectGather:
    def __init__(self, count, own, slots, send_sem, recv_sem):
        self.count, self.own, self.slots = count, own, slots
        self.send_sem, self.recv_sem = send_sem, recv_sem
        self.me = lax.axis_index("band")
        self.spin = lax.axis_index("spin")

    def copy(self, block, target):
        return pltpu.make_async_remote_copy(
            src_ref=self.own,
            dst_ref=self.slots.at[block],
            send_sem=self.send_sem.at[target],
            recv_sem=self.recv_sem.at[0, block],
            device_id=(self.spin, target),
            device_id_type=MESH,
        )

    def each(self, action):
        def step(k, carry):
            action(lax.rem(self.me + k, self.count))
            return carry

        lax.fori_loop(1, self.count, step, 0)

    def send_own(self):
        self.each(lambda other: self.copy(self.me, other).start())

    def take_all(self):
        self.each(lambda other: self.copy(other, other).wait_recv())

    def finish(self):
        self.each(lambda other: self.copy(self.me, other).wait_send())


def relayed(count, sizes):
    return math.prod(len(offsets_of(s)) for s in sizes) <= 64 and count > 1


def kernel(
    count, spins, points,
    own, potential, row_factor, column_factor, left_high, left_low, green, wave,
    updated, residual,
    slots, table_high, table_low, density, other_density, cube, flat,
    send_sem, recv_sem, swap_sem,
):
    volume = points**3
    plane = points * points
    blocks = plane // LANES
    sizes = line_sizes(count)
    me = lax.axis_index("band")
    spin = lax.axis_index("spin")
    relay = relayed(count, sizes)

    barrier = pltpu.get_barrier_semaphore()
    expected = jnp.int32(0)
    if relay:
        gather = Gather(count, sizes, own, slots, send_sem, recv_sem)
        for ok, target in gather.neighbours():
            def greet(target=target):
                pl.semaphore_signal(barrier, inc=1, device_id=(spin, target), device_id_type=MESH)

            if ok is None:
                greet()
                expected = expected + 1
            else:
                pl.when(ok)(greet)
                expected = expected + ok.astype(jnp.int32)
    else:
        gather = DirectGather(count, own, slots, send_sem, recv_sem)
        gather.each(
            lambda other: pl.semaphore_signal(barrier, inc=1, device_id=(spin, other), device_id_type=MESH)
        )
        expected = expected + (count - 1)
    for away in range(1, spins):
        pl.semaphore_signal(
            barrier, inc=1, device_id=(lax.rem(spin + away, spins), me), device_id_type=MESH
        )
    pl.semaphore_wait(barrier, expected + (spins - 1))
    gather.send_own()

    def build(y, carry):
        rows = pl.ds(pl.multiple_of(y * points, points), points)
        high, low = bf16_split(row_factor[pl.ds(y, 1), :] * column_factor[...])
        table_high[rows, :] = high
        table_low[rows, :] = low
        return carry

    lax.fori_loop(0, points, build, 0)

    def as_cube(ref):
        return jnp.concatenate(
            [ref[pl.ds(k, points, stride=blocks), :] for k in range(blocks)], axis=1
        )

    def transform(fields):
        rows = fields.shape[0]
        high, low = bf16_split(fields)
        lh, ll = left_high[:rows, :rows], left_low[:rows, :rows]
        turned = dot(lh, high) + dot(lh, low) + dot(ll, high)
        high, low = bf16_split(turned)
        both = dot(jnp.concatenate([high, low], axis=0), table_high[...])
        return both[:rows] + both[rows:] + dot(high, table_low[...])

    def scaled(fields, factors):
        return jnp.concatenate(
            [fields[k * points : (k + 1) * points] * f for k, f in enumerate(factors)], axis=0
        )

    resident = as_cube(own)
    slots[me] = own[...]
    first = transform(jnp.concatenate([resident, resident * resident], axis=0))
    first = transform(scaled(first, (wave[...], green[...])))
    cube[...] = first[:points] - mixing * (first[points:] * resident)

    if relay:
        for _, half, offsets in gather.events():
            gather.take(half, offsets)
    else:
        gather.take_all()

    def add_square(j, total):
        band = slots[j]
        return total + band * band

    density[...] = lax.fori_loop(0, count, add_square, jnp.zeros(own.shape, jnp.float32))
    swaps = []
    for away in range(1, spins):
        swap = pltpu.make_async_remote_copy(
            src_ref=density,
            dst_ref=other_density.at[away - 1],
            send_sem=swap_sem.at[0, away - 1],
            recv_sem=swap_sem.at[1, away - 1],
            device_id=(lax.rem(spin + away, spins), me),
            device_id_type=MESH,
        )
        swap.start()
        swaps.append(swap)

    partners = [as_cube(slots.at[lax.rem(me + o + count, count)]) for o in (1, 2, -1, -2)]
    fields = transform(jnp.concatenate([resident * p for p in partners], axis=0))
    fields = transform(scaled(fields, (green[...],) * len(partners)))
    exchange = cube[...]
    for k, p in enumerate(partners):
        exchange = exchange - mixing * (fields[k * points : (k + 1) * points] * p)

    for swap in swaps:
        swap.wait()
    total = as_cube(density)
    for away in range(1, spins):
        total = total + as_cube(other_density.at[away - 1])
    screened = transform(transform(total) * green[...])
    local = as_cube(potential) + hartree_weight * screened
    gradient = exchange + local * resident
    for k in range(blocks):
        flat[pl.ds(k, points, stride=blocks), :] = gradient[:, k * LANES : (k + 1) * LANES]

    def project(values):
        def step(j, left):
            band = slots[j]
            share = jnp.sum(jnp.sum(band * values, axis=0, keepdims=True), axis=1, keepdims=True)
            return left - (share / volume) * band

        return lax.fori_loop(0, count, step, values)

    flat[...] = project(flat[...])
    result = project(flat[...])
    residual[...] = result
    updated[...] = own[...] - step_length * result
    gather.finish()


def tables(points, batch):
    indices = np.arange(points)
    angles = (indices[:, None] * indices[None, :] % points) * (2.0 * math.pi / points)
    table = (np.cos(angles) + np.sin(angles)).astype(np.float32)
    left = np.kron(np.eye(batch, dtype=np.float32), table)
    folded = np.where(indices < points // 2, indices, indices - points) * (math.pi / points)
    square = folded * folded
    summed = square[:, None, None] + square[None, :, None] + square[None, None, :]
    summed = summed.reshape(points, points * points)
    volume = points**3
    green = np.where(summed > 0, 1.0 / (summed + screen_square), 0.0) / volume
    wave = 0.5 * summed / volume
    return (
        np.repeat(table, points, axis=1),
        np.tile(table, (1, points)),
        left,
        green.astype(np.float32),
        wave.astype(np.float32),
    )


def per_device(count, spins, orbitals, potential):
    volume = orbitals.shape[2]
    points = round(volume ** (1 / 3))
    rows = volume // LANES
    row_factor, column_factor, left, green, wave = tables(points, 4)
    left_high = left.astype(jnp.bfloat16)
    left_low = (left - left_high.astype(np.float32)).astype(jnp.bfloat16)
    sizes = line_sizes(count)
    if relayed(count, sizes):
        sends = 12 + 4 * 2 * math.prod(len(offsets_of(s)) for s in sizes)
    else:
        sends = count
    vmem = pl.BlockSpec(memory_space=pltpu.VMEM)
    flat_shape = jax.ShapeDtypeStruct((rows, LANES), jnp.float32)
    updated, residual = pl.pallas_call(
        functools.partial(kernel, count, spins, points),
        out_shape=(flat_shape, flat_shape),
        in_specs=[vmem] * 8,
        out_specs=(vmem, vmem),
        scratch_shapes=[
            pltpu.VMEM((count, rows, LANES), jnp.float32),
            pltpu.VMEM((points * points, points * points), jnp.bfloat16),
            pltpu.VMEM((points * points, points * points), jnp.bfloat16),
            pltpu.VMEM((rows, LANES), jnp.float32),
            pltpu.VMEM((max(spins - 1, 1), rows, LANES), jnp.float32),
            pltpu.VMEM((points, points * points), jnp.float32),
            pltpu.VMEM((rows, LANES), jnp.float32),
            pltpu.SemaphoreType.DMA((sends,)),
            pltpu.SemaphoreType.DMA((2, count)),
            pltpu.SemaphoreType.DMA((2, max(spins - 1, 1))),
        ],
        compiler_params=pltpu.CompilerParams(
            collective_id=0, has_side_effects=True, vmem_limit_bytes=60 * 1024 * 1024
        ),
    )(
        orbitals.reshape(rows, LANES), potential.reshape(rows, LANES),
        row_factor, column_factor, left_high, left_low, green, wave,
    )
    return updated.reshape(orbitals.shape), residual.reshape(orbitals.shape)


def solution(mesh):
    return jax.shard_map(
        functools.partial(per_device, mesh.shape["band"], mesh.shape["spin"]),
        mesh=mesh,
        in_specs=(P("spin", "band", None), P()),
        out_specs=(P("spin", "band", None), P("spin", "band", None)),
        check_vma=False,
    )
```

```python
import functools
import math

import jax
import jax.numpy as jnp
import numpy as np
from jax import lax
from jax.experimental import pallas as pl
from jax.experimental.pallas import tpu as pltpu
from jax.sharding import PartitionSpec as P

screen_square = 0.04
hartree_weight = 0.03125
mixing = 0.25
step_length = 0.1

MESH = pl.DeviceIdType.MESH
LANES = 128
PARTS = (((0, 1, 2), 16), ((0, 2, 1), 16))
PART_UNITS = sum(share for _, share in PARTS)


def line_sizes(count):
    power = int(math.log2(count)) if count > 1 else 0
    if 2**power != count:
        return (count, 1, 1)
    fast = 2 ** (power // 3)
    return (count // (fast * fast), fast, fast)


def offsets_of(size):
    if size == 1:
        return (0,)
    if size == 2:
        return (0, 1)
    return tuple(range(-(size - 1), size))


def bf16_split(x):
    high = x.astype(jnp.bfloat16)
    return high, (x - high.astype(jnp.float32)).astype(jnp.bfloat16)


def dot(a, b):
    return jnp.dot(a, b, preferred_element_type=jnp.float32)


class Gather:
    def __init__(self, count, sizes, own, slots, send_sem, recv_sem):
        self.count, self.sizes, self.own, self.slots = count, sizes, own, slots
        self.send_sem, self.recv_sem = send_sem, recv_sem
        rows = own.shape[0]
        bounds = [0]
        for _, share in PARTS:
            bounds.append(bounds[-1] + rows * share // PART_UNITS)
        bounds[-1] = rows
        self.bounds = bounds
        self.me = lax.axis_index("band")
        self.spin = lax.axis_index("spin")
        strides = (sizes[1] * sizes[2], sizes[2], 1)
        self.strides = strides
        self.coords = tuple(lax.rem(self.me // strides[d], sizes[d]) for d in range(3))
        self.sent = []

    def neighbours(self):
        found = []
        for d in range(3):
            for way in self.ways(d):
                found.append(self.neighbour(d, way))
        return found

    def ways(self, d):
        return () if self.sizes[d] == 1 else (1,) if self.sizes[d] == 2 else (1, -1)

    def neighbour(self, d, way):
        c = self.coords[d]
        if self.sizes[d] == 2:
            return None, self.me + (1 - 2 * c) * self.strides[d]
        guard = c + way < self.sizes[d] if way > 0 else c + way >= 0
        return guard, self.me + way * self.strides[d]

    def part(self, half):
        return pl.ds(self.bounds[half], self.bounds[half + 1] - self.bounds[half])

    def send(self, half, block, d, way, guard):
        ok, target = self.neighbour(d, way)
        if guard is not None:
            ok = guard if ok is None else jnp.logical_and(ok, guard)
        copy = pltpu.make_async_remote_copy(
            src_ref=self.slots.at[block, self.part(half)],
            dst_ref=self.slots.at[block, self.part(half)],
            send_sem=self.send_sem.at[len(self.sent)],
            recv_sem=self.recv_sem.at[half, block],
            device_id=(self.spin, target),
            device_id_type=MESH,
        )
        self.sent.append((ok, copy))
        if ok is None:
            copy.start()
        else:
            pl.when(ok)(copy.start)

    def order(self, half):
        return PARTS[half][0]

    def send_own(self):
        for step in range(3):
            for half in reversed(range(len(PARTS))):
                d = self.order(half)[step]
                for way in self.ways(d):
                    self.send(half, self.me, d, way, None)

    def events(self):
        found = []
        for half in range(len(PARTS)):
            for z in offsets_of(self.sizes[0]):
                for y in offsets_of(self.sizes[1]):
                    for x in offsets_of(self.sizes[2]):
                        if (z, y, x) != (0, 0, 0):
                            found.append((abs(z) + abs(y) + abs(x), half, (z, y, x)))
        found = sorted(found, key=lambda e: (e[0], -e[1], -abs(e[2][0])))
        onward = [e[1:] for e in found if not self.ends(*e[1:])]
        return onward, [e[1:] for e in found if self.ends(*e[1:])]

    def ends(self, half, offsets):
        d = self.order(half)[2]
        o = offsets[d]
        return o != 0 and (self.sizes[d] <= 2 or abs(o) == self.sizes[d] - 1)

    def take(self, half, offsets):
        guard, block = None, self.me
        for d, o in enumerate(offsets):
            if o == 0:
                continue
            c = self.coords[d]
            if self.sizes[d] == 2:
                block = block + (1 - 2 * c) * self.strides[d]
            else:
                ok = c + o < self.sizes[d] if o > 0 else c + o >= 0
                guard = ok if guard is None else jnp.logical_and(guard, ok)
                block = block + o * self.strides[d]
        if guard is not None:
            block = jnp.where(guard, block, self.me)
        arrived = self.slots.at[block, self.part(half)]
        wait = pltpu.make_async_remote_copy(
            src_ref=arrived,
            dst_ref=arrived,
            send_sem=self.send_sem.at[0],
            recv_sem=self.recv_sem.at[half, block],
            device_id=(self.spin, self.me),
            device_id_type=MESH,
        ).wait_recv
        if guard is None:
            wait()
        else:
            pl.when(guard)(wait)
        order = self.order(half)
        last = max(p for p in range(3) if offsets[order[p]] != 0)
        d = order[last]
        if self.sizes[d] > 2:
            self.send(half, block, d, -1 if offsets[d] > 0 else 1, guard)
        for later in order[last + 1 :]:
            for way in self.ways(later):
                self.send(half, block, later, way, guard)

    def finish(self):
        for ok, copy in self.sent:
            if ok is None:
                copy.wait_send()
            else:
                pl.when(ok)(copy.wait_send)


class DirectGather:
    def __init__(self, count, own, slots, send_sem, recv_sem):
        self.count, self.own, self.slots = count, own, slots
        self.send_sem, self.recv_sem = send_sem, recv_sem
        self.me = lax.axis_index("band")
        self.spin = lax.axis_index("spin")

    def copy(self, block, target):
        return pltpu.make_async_remote_copy(
            src_ref=self.own,
            dst_ref=self.slots.at[block],
            send_sem=self.send_sem.at[target],
            recv_sem=self.recv_sem.at[0, block],
            device_id=(self.spin, target),
            device_id_type=MESH,
        )

    def each(self, action):
        def step(k, carry):
            action(lax.rem(self.me + k, self.count))
            return carry

        lax.fori_loop(1, self.count, step, 0)

    def send_own(self):
        self.each(lambda other: self.copy(self.me, other).start())

    def take_all(self):
        self.each(lambda other: self.copy(other, other).wait_recv())

    def finish(self):
        self.each(lambda other: self.copy(self.me, other).wait_send())


def relayed(count, sizes):
    return math.prod(len(offsets_of(s)) for s in sizes) <= 64 and count > 1


def kernel(
    count, spins, points,
    own_hbm, potential_hbm, row_hbm, column_hbm, left_high_hbm, left_low_hbm, green_hbm, wave_hbm,
    negative,
    slots, table_high, table_low, density, other_density, cube, flat, parts,
    potential, row_factor, column_factor, left_high, left_low, green, wave,
    send_sem, recv_sem, swap_sem, load_sem,
):
    volume = points**3
    plane = points * points
    blocks = plane // LANES
    sizes = line_sizes(count)
    me = lax.axis_index("band")
    spin = lax.axis_index("spin")
    relay = relayed(count, sizes)

    own = slots.at[me]
    loads = [
        pltpu.make_async_copy(source, target, load_sem.at[k])
        for k, (source, target) in enumerate(
            (
                (own_hbm, own), (row_hbm, row_factor), (column_hbm, column_factor),
                (left_high_hbm, left_high), (left_low_hbm, left_low), (green_hbm, green),
                (wave_hbm, wave), (potential_hbm, potential),
            )
        )
    ]
    for load in loads:
        load.start()

    barrier = pltpu.get_barrier_semaphore()
    expected = jnp.int32(0)
    if relay:
        gather = Gather(count, sizes, own, slots, send_sem, recv_sem)
        for ok, target in gather.neighbours():
            def greet(target=target):
                pl.semaphore_signal(barrier, inc=1, device_id=(spin, target), device_id_type=MESH)

            if ok is None:
                greet()
                expected = expected + 1
            else:
                pl.when(ok)(greet)
                expected = expected + ok.astype(jnp.int32)
    else:
        gather = DirectGather(count, own, slots, send_sem, recv_sem)
        gather.each(
            lambda other: pl.semaphore_signal(barrier, inc=1, device_id=(spin, other), device_id_type=MESH)
        )
        expected = expected + (count - 1)
    for away in range(1, spins):
        pl.semaphore_signal(
            barrier, inc=1, device_id=(lax.rem(spin + away, spins), me), device_id_type=MESH
        )
    loads[0].wait()
    pl.semaphore_wait(barrier, expected + (spins - 1))
    gather.send_own()
    for load in loads[1:]:
        load.wait()

    def build(y, carry):
        rows = pl.ds(pl.multiple_of(y * points, points), points)
        high, low = bf16_split(row_factor[pl.ds(y, 1), :] * column_factor[...])
        table_high[rows, :] = high
        table_low[rows, :] = low
        return carry

    lax.fori_loop(0, points, build, 0)

    def as_cube(ref):
        return jnp.concatenate(
            [ref[pl.ds(k, points, stride=blocks), :] for k in range(blocks)], axis=1
        )

    def transform(fields):
        rows = fields.shape[0]
        high, low = bf16_split(fields)
        lh, ll = left_high[:rows, :rows], left_low[:rows, :rows]
        turned = dot(lh, high) + dot(lh, low) + dot(ll, high)
        high, low = bf16_split(turned)
        both = dot(jnp.concatenate([high, low], axis=0), table_high[...])
        return both[:rows] + both[rows:] + dot(high, table_low[...])

    def scaled(fields, factors):
        return jnp.concatenate(
            [fields[k * points : (k + 1) * points] * f for k, f in enumerate(factors)], axis=0
        )

    if relay:
        onward, ending = gather.events()
        for half, offsets in onward:
            gather.take(half, offsets)

    resident = as_cube(own)
    first = transform(jnp.concatenate([resident, resident * resident], axis=0))
    first = transform(scaled(first, (wave[...], green[...])))
    cube[...] = first[:points] - mixing * (first[points:] * resident)

    if relay:
        for half, offsets in ending:
            gather.take(half, offsets)
    else:
        gather.take_all()
    unroll = count if count <= 16 else 1

    def add_square(j, total):
        band = slots[j]
        return total + band * band

    density[...] = lax.fori_loop(
        0, count, add_square, jnp.zeros(density.shape, jnp.float32), unroll=unroll
    )
    swaps = []
    for away in range(1, spins):
        swap = pltpu.make_async_remote_copy(
            src_ref=density,
            dst_ref=other_density.at[away - 1],
            send_sem=swap_sem.at[0, away - 1],
            recv_sem=swap_sem.at[1, away - 1],
            device_id=(lax.rem(spin + away, spins), me),
            device_id_type=MESH,
        )
        swap.start()
        swaps.append(swap)

    partners = [as_cube(slots.at[lax.rem(me + o + count, count)]) for o in (1, 2, -1, -2)]
    fields = transform(jnp.concatenate([resident * p for p in partners], axis=0))
    fields = transform(scaled(fields, (green[...],) * len(partners)))
    exchange = cube[...]
    for k, p in enumerate(partners):
        exchange = exchange - mixing * (fields[k * points : (k + 1) * points] * p)

    for swap in swaps:
        swap.wait()
    total = as_cube(density)
    for away in range(1, spins):
        total = total + as_cube(other_density.at[away - 1])
    screened = transform(transform(total) * green[...])
    local = as_cube(potential) + hartree_weight * screened
    gradient = exchange + local * resident
    for k in range(blocks):
        flat[pl.ds(k, points, stride=blocks), :] = gradient[:, k * LANES : (k + 1) * LANES]

    def project(values):
        def overlap(j, carry):
            parts[pl.ds(j, 1), :] = jnp.sum(slots[j] * values, axis=0, keepdims=True)
            return carry

        lax.fori_loop(0, count, overlap, 0, unroll=unroll)
        shares = jnp.sum(parts[...], axis=1, keepdims=True) / volume
        parts[...] = jnp.broadcast_to(shares, parts.shape)
        return lax.fori_loop(
            0, count, lambda j, left: left - parts[pl.ds(j, 1), :] * slots[j], values, unroll=unroll
        )

    negative[...] = -project(project(flat[...]))
    gather.finish()


def tables(points, batch):
    indices = np.arange(points)
    angles = (indices[:, None] * indices[None, :] % points) * (2.0 * math.pi / points)
    table = (np.cos(angles) + np.sin(angles)).astype(np.float32)
    left = np.kron(np.eye(batch, dtype=np.float32), table)
    folded = np.where(indices < points // 2, indices, indices - points) * (math.pi / points)
    square = folded * folded
    summed = square[:, None, None] + square[None, :, None] + square[None, None, :]
    summed = summed.reshape(points, points * points)
    volume = points**3
    green = np.where(summed > 0, 1.0 / (summed + screen_square), 0.0) / volume
    wave = 0.5 * summed / volume
    return (
        np.repeat(table, points, axis=1),
        np.tile(table, (1, points)),
        left,
        green.astype(np.float32),
        wave.astype(np.float32),
    )


def per_device(count, spins, orbitals, potential):
    volume = orbitals.shape[2]
    points = round(volume ** (1 / 3))
    rows = volume // LANES
    row_factor, column_factor, left, green, wave = tables(points, 4)
    left_high = left.astype(jnp.bfloat16)
    left_low = (left - left_high.astype(np.float32)).astype(jnp.bfloat16)
    sizes = line_sizes(count)
    if relayed(count, sizes):
        sends = 12 * len(PARTS) + 4 * len(PARTS) * math.prod(len(offsets_of(s)) for s in sizes)
    else:
        sends = count
    constants = (row_factor, column_factor, left_high, left_low, green, wave)
    negative = pl.pallas_call(
        functools.partial(kernel, count, spins, points),
        out_shape=jax.ShapeDtypeStruct((rows, LANES), jnp.float32),
        in_specs=[pl.BlockSpec(memory_space=pl.ANY)] * 8,
        out_specs=pl.BlockSpec(memory_space=pltpu.VMEM),
        scratch_shapes=[
            pltpu.VMEM((count, rows, LANES), jnp.float32),
            pltpu.VMEM((points * points, points * points), jnp.bfloat16),
            pltpu.VMEM((points * points, points * points), jnp.bfloat16),
            pltpu.VMEM((rows, LANES), jnp.float32),
            pltpu.VMEM((max(spins - 1, 1), rows, LANES), jnp.float32),
            pltpu.VMEM((points, points * points), jnp.float32),
            pltpu.VMEM((rows, LANES), jnp.float32),
            pltpu.VMEM((count, LANES), jnp.float32),
            pltpu.VMEM((rows, LANES), jnp.float32),
        ]
        + [pltpu.VMEM(c.shape, c.dtype) for c in constants]
        + [
            pltpu.SemaphoreType.DMA((sends,)),
            pltpu.SemaphoreType.DMA((len(PARTS), count)),
            pltpu.SemaphoreType.DMA((2, max(spins - 1, 1))),
            pltpu.SemaphoreType.DMA((8,)),
        ],
        compiler_params=pltpu.CompilerParams(
            collective_id=0,
            has_side_effects=True,
            vmem_limit_bytes=60 * 1024 * 1024,
        ),
    )(orbitals.reshape(rows, LANES), potential.reshape(rows, LANES), *constants)
    updated = orbitals.reshape(rows, LANES) + step_length * negative
    return updated.reshape(orbitals.shape), (-negative).reshape(orbitals.shape)


def solution(mesh):
    return jax.shard_map(
        functools.partial(per_device, mesh.shape["band"], mesh.shape["spin"]),
        mesh=mesh,
        in_specs=(P("spin", "band", None), P()),
        out_specs=(P("spin", "band", None), P("spin", "band", None)),
        check_vma=False,
    )
```

```python
import functools
import math

import jax
import jax.numpy as jnp
import numpy as np
from jax import lax
from jax.experimental import pallas as pl
from jax.experimental.pallas import tpu as pltpu
from jax.sharding import PartitionSpec as P

screen_square = 0.04
hartree_weight = 0.03125
mixing = 0.25
step_length = 0.1

MESH = pl.DeviceIdType.MESH
LANES = 128
PARTS = (((0, 1, 2), 16), ((0, 2, 1), 16))
PART_UNITS = sum(share for _, share in PARTS)


def line_sizes(count):
    power = int(math.log2(count)) if count > 1 else 0
    if 2**power != count:
        return (count, 1, 1)
    fast = 2 ** (power // 3)
    return (count // (fast * fast), fast, fast)


def offsets_of(size):
    if size == 1:
        return (0,)
    if size == 2:
        return (0, 1)
    return tuple(range(-(size - 1), size))


def bf16_split(x):
    high = x.astype(jnp.bfloat16)
    return high, (x - high.astype(jnp.float32)).astype(jnp.bfloat16)


def dot(a, b):
    return jnp.dot(a, b, preferred_element_type=jnp.float32)


class Gather:
    def __init__(self, count, sizes, own, slots, send_sem, recv_sem):
        self.count, self.sizes, self.own, self.slots = count, sizes, own, slots
        self.send_sem, self.recv_sem = send_sem, recv_sem
        rows = own.shape[0]
        bounds = [0]
        for _, share in PARTS:
            bounds.append(bounds[-1] + rows * share // PART_UNITS)
        bounds[-1] = rows
        self.bounds = bounds
        self.me = lax.axis_index("band")
        self.spin = lax.axis_index("spin")
        strides = (sizes[1] * sizes[2], sizes[2], 1)
        self.strides = strides
        self.coords = tuple(lax.rem(self.me // strides[d], sizes[d]) for d in range(3))
        self.sent = []

    def neighbours(self):
        found = []
        for d in range(3):
            for way in self.ways(d):
                found.append(self.neighbour(d, way))
        return found

    def ways(self, d):
        return () if self.sizes[d] == 1 else (1,) if self.sizes[d] == 2 else (1, -1)

    def neighbour(self, d, way):
        c = self.coords[d]
        if self.sizes[d] == 2:
            return None, self.me + (1 - 2 * c) * self.strides[d]
        guard = c + way < self.sizes[d] if way > 0 else c + way >= 0
        return guard, self.me + way * self.strides[d]

    def part(self, half):
        return pl.ds(self.bounds[half], self.bounds[half + 1] - self.bounds[half])

    def send(self, half, block, d, way, guard):
        ok, target = self.neighbour(d, way)
        if guard is not None:
            ok = guard if ok is None else jnp.logical_and(ok, guard)
        copy = pltpu.make_async_remote_copy(
            src_ref=self.slots.at[block, self.part(half)],
            dst_ref=self.slots.at[block, self.part(half)],
            send_sem=self.send_sem.at[len(self.sent)],
            recv_sem=self.recv_sem.at[half, block],
            device_id=(self.spin, target),
            device_id_type=MESH,
        )
        self.sent.append((ok, copy))
        if ok is None:
            copy.start()
        else:
            pl.when(ok)(copy.start)

    def order(self, half):
        return PARTS[half][0]

    def send_own(self):
        for step in range(3):
            for half in reversed(range(len(PARTS))):
                d = self.order(half)[step]
                for way in self.ways(d):
                    self.send(half, self.me, d, way, None)

    def events(self):
        found = []
        for half in range(len(PARTS)):
            for z in offsets_of(self.sizes[0]):
                for y in offsets_of(self.sizes[1]):
                    for x in offsets_of(self.sizes[2]):
                        if (z, y, x) != (0, 0, 0):
                            found.append((abs(z) + abs(y) + abs(x), half, (z, y, x)))
        found = sorted(found, key=lambda e: (e[2][1] + e[2][2], abs(e[2][0]), -e[1]))
        onward = [e[1:] for e in found if not self.ends(*e[1:])]
        return onward, [e[1:] for e in found if self.ends(*e[1:])]

    def ends(self, half, offsets):
        d = self.order(half)[2]
        o = offsets[d]
        return o != 0 and (self.sizes[d] <= 2 or abs(o) == self.sizes[d] - 1)

    def take(self, half, offsets):
        guard, block = None, self.me
        for d, o in enumerate(offsets):
            if o == 0:
                continue
            c = self.coords[d]
            if self.sizes[d] == 2:
                block = block + (1 - 2 * c) * self.strides[d]
            else:
                ok = c + o < self.sizes[d] if o > 0 else c + o >= 0
                guard = ok if guard is None else jnp.logical_and(guard, ok)
                block = block + o * self.strides[d]
        if guard is not None:
            block = jnp.where(guard, block, self.me)
        arrived = self.slots.at[block, self.part(half)]
        wait = pltpu.make_async_remote_copy(
            src_ref=arrived,
            dst_ref=arrived,
            send_sem=self.send_sem.at[0],
            recv_sem=self.recv_sem.at[half, block],
            device_id=(self.spin, self.me),
            device_id_type=MESH,
        ).wait_recv
        if guard is None:
            wait()
        else:
            pl.when(guard)(wait)
        order = self.order(half)
        last = max(p for p in range(3) if offsets[order[p]] != 0)
        d = order[last]
        if self.sizes[d] > 2:
            self.send(half, block, d, -1 if offsets[d] > 0 else 1, guard)
        for later in order[last + 1 :]:
            for way in self.ways(later):
                self.send(half, block, later, way, guard)

    def finish(self):
        for ok, copy in self.sent:
            if ok is None:
                copy.wait_send()
            else:
                pl.when(ok)(copy.wait_send)


class DirectGather:
    def __init__(self, count, own, slots, send_sem, recv_sem):
        self.count, self.own, self.slots = count, own, slots
        self.send_sem, self.recv_sem = send_sem, recv_sem
        self.me = lax.axis_index("band")
        self.spin = lax.axis_index("spin")

    def copy(self, block, target):
        return pltpu.make_async_remote_copy(
            src_ref=self.own,
            dst_ref=self.slots.at[block],
            send_sem=self.send_sem.at[target],
            recv_sem=self.recv_sem.at[0, block],
            device_id=(self.spin, target),
            device_id_type=MESH,
        )

    def each(self, action):
        def step(k, carry):
            action(lax.rem(self.me + k, self.count))
            return carry

        lax.fori_loop(1, self.count, step, 0)

    def send_own(self):
        self.each(lambda other: self.copy(self.me, other).start())

    def take_all(self):
        self.each(lambda other: self.copy(other, other).wait_recv())

    def finish(self):
        self.each(lambda other: self.copy(self.me, other).wait_send())


def relayed(count, sizes):
    return math.prod(len(offsets_of(s)) for s in sizes) <= 64 and count > 1


def kernel(
    count, spins, points,
    own_hbm, potential_hbm, row_hbm, column_hbm, left_high_hbm, left_low_hbm, green_hbm, wave_hbm,
    negative,
    slots, table_high, table_low, density, other_density, cube, flat, parts,
    potential, row_factor, column_factor, left_high, left_low, green, wave,
    send_sem, recv_sem, swap_sem, load_sem,
):
    volume = points**3
    plane = points * points
    blocks = plane // LANES
    sizes = line_sizes(count)
    me = lax.axis_index("band")
    spin = lax.axis_index("spin")
    relay = relayed(count, sizes)

    own = slots.at[me]
    loads = [
        pltpu.make_async_copy(source, target, load_sem.at[k])
        for k, (source, target) in enumerate(
            (
                (own_hbm, own), (row_hbm, row_factor), (column_hbm, column_factor),
                (left_high_hbm, left_high), (left_low_hbm, left_low), (green_hbm, green),
                (wave_hbm, wave), (potential_hbm, potential),
            )
        )
    ]
    for load in loads:
        load.start()

    barrier = pltpu.get_barrier_semaphore()
    expected = jnp.int32(0)
    if relay:
        gather = Gather(count, sizes, own, slots, send_sem, recv_sem)
        for ok, target in gather.neighbours():
            def greet(target=target):
                pl.semaphore_signal(barrier, inc=1, device_id=(spin, target), device_id_type=MESH)

            if ok is None:
                greet()
                expected = expected + 1
            else:
                pl.when(ok)(greet)
                expected = expected + ok.astype(jnp.int32)
    else:
        gather = DirectGather(count, own, slots, send_sem, recv_sem)
        gather.each(
            lambda other: pl.semaphore_signal(barrier, inc=1, device_id=(spin, other), device_id_type=MESH)
        )
        expected = expected + (count - 1)
    for away in range(1, spins):
        pl.semaphore_signal(
            barrier, inc=1, device_id=(lax.rem(spin + away, spins), me), device_id_type=MESH
        )
    loads[0].wait()
    pl.semaphore_wait(barrier, expected + (spins - 1))
    gather.send_own()
    for load in loads[1:]:
        load.wait()

    def build(y, carry):
        rows = pl.ds(pl.multiple_of(y * points, points), points)
        high, low = bf16_split(row_factor[pl.ds(y, 1), :] * column_factor[...])
        table_high[rows, :] = high
        table_low[rows, :] = low
        return carry

    lax.fori_loop(0, points, build, 0)

    def as_cube(ref):
        return jnp.concatenate(
            [ref[pl.ds(k, points, stride=blocks), :] for k in range(blocks)], axis=1
        )

    def transform(fields):
        rows = fields.shape[0]
        high, low = bf16_split(fields)
        lh, ll = left_high[:rows, :rows], left_low[:rows, :rows]
        turned = dot(lh, high) + dot(lh, low) + dot(ll, high)
        high, low = bf16_split(turned)
        both = dot(jnp.concatenate([high, low], axis=0), table_high[...])
        return both[:rows] + both[rows:] + dot(high, table_low[...])

    def scaled(fields, factors):
        return jnp.concatenate(
            [fields[k * points : (k + 1) * points] * f for k, f in enumerate(factors)], axis=0
        )

    if relay:
        onward, ending = gather.events()
        for half, offsets in onward:
            gather.take(half, offsets)

    resident = as_cube(own)
    first = transform(jnp.concatenate([resident, resident * resident], axis=0))
    first = transform(scaled(first, (wave[...], green[...])))
    cube[...] = first[:points] - mixing * (first[points:] * resident)

    if relay:
        for half, offsets in ending:
            gather.take(half, offsets)
    else:
        gather.take_all()
    unroll = count if count <= 16 else 1

    def add_square(j, total):
        band = slots[j]
        return total + band * band

    density[...] = lax.fori_loop(
        0, count, add_square, jnp.zeros(density.shape, jnp.float32), unroll=unroll
    )
    swaps = []
    for away in range(1, spins):
        swap = pltpu.make_async_remote_copy(
            src_ref=density,
            dst_ref=other_density.at[away - 1],
            send_sem=swap_sem.at[0, away - 1],
            recv_sem=swap_sem.at[1, away - 1],
            device_id=(lax.rem(spin + away, spins), me),
            device_id_type=MESH,
        )
        swap.start()
        swaps.append(swap)

    partners = [as_cube(slots.at[lax.rem(me + o + count, count)]) for o in (1, 2, -1, -2)]
    for swap in swaps:
        swap.wait()
    total = as_cube(density)
    for away in range(1, spins):
        total = total + as_cube(other_density.at[away - 1])
    fields = transform(jnp.concatenate([resident * p for p in partners] + [total], axis=0))
    fields = transform(scaled(fields, (green[...],) * (len(partners) + 1)))
    exchange = cube[...]
    for k, p in enumerate(partners):
        exchange = exchange - mixing * (fields[k * points : (k + 1) * points] * p)
    screened = fields[len(partners) * points :]
    local = as_cube(potential) + hartree_weight * screened
    gradient = exchange + local * resident
    for k in range(blocks):
        flat[pl.ds(k, points, stride=blocks), :] = gradient[:, k * LANES : (k + 1) * LANES]

    def project(values):
        def overlap(j, carry):
            parts[pl.ds(j, 1), :] = jnp.sum(slots[j] * values, axis=0, keepdims=True)
            return carry

        lax.fori_loop(0, count, overlap, 0, unroll=unroll)
        shares = jnp.sum(parts[...], axis=1, keepdims=True) / volume
        parts[...] = jnp.broadcast_to(shares, parts.shape)
        return lax.fori_loop(
            0, count, lambda j, left: left - parts[pl.ds(j, 1), :] * slots[j], values, unroll=unroll
        )

    negative[...] = -project(project(flat[...]))
    gather.finish()


def tables(points, batch):
    indices = np.arange(points)
    angles = (indices[:, None] * indices[None, :] % points) * (2.0 * math.pi / points)
    table = (np.cos(angles) + np.sin(angles)).astype(np.float32)
    left = np.kron(np.eye(batch, dtype=np.float32), table)
    folded = np.where(indices < points // 2, indices, indices - points) * (math.pi / points)
    square = folded * folded
    summed = square[:, None, None] + square[None, :, None] + square[None, None, :]
    summed = summed.reshape(points, points * points)
    volume = points**3
    green = np.where(summed > 0, 1.0 / (summed + screen_square), 0.0) / volume
    wave = 0.5 * summed / volume
    return (
        np.repeat(table, points, axis=1),
        np.tile(table, (1, points)),
        left,
        green.astype(np.float32),
        wave.astype(np.float32),
    )


def per_device(count, spins, orbitals, potential):
    volume = orbitals.shape[2]
    points = round(volume ** (1 / 3))
    rows = volume // LANES
    row_factor, column_factor, left, green, wave = tables(points, 5)
    left_high = left.astype(jnp.bfloat16)
    left_low = (left - left_high.astype(np.float32)).astype(jnp.bfloat16)
    sizes = line_sizes(count)
    if relayed(count, sizes):
        sends = 12 * len(PARTS) + 4 * len(PARTS) * math.prod(len(offsets_of(s)) for s in sizes)
    else:
        sends = count
    constants = (row_factor, column_factor, left_high, left_low, green, wave)
    negative = pl.pallas_call(
        functools.partial(kernel, count, spins, points),
        out_shape=jax.ShapeDtypeStruct((rows, LANES), jnp.float32),
        in_specs=[pl.BlockSpec(memory_space=pl.ANY)] * 8,
        out_specs=pl.BlockSpec(memory_space=pltpu.VMEM),
        scratch_shapes=[
            pltpu.VMEM((count, rows, LANES), jnp.float32),
            pltpu.VMEM((points * points, points * points), jnp.bfloat16),
            pltpu.VMEM((points * points, points * points), jnp.bfloat16),
            pltpu.VMEM((rows, LANES), jnp.float32),
            pltpu.VMEM((max(spins - 1, 1), rows, LANES), jnp.float32),
            pltpu.VMEM((points, points * points), jnp.float32),
            pltpu.VMEM((rows, LANES), jnp.float32),
            pltpu.VMEM((count, LANES), jnp.float32),
            pltpu.VMEM((rows, LANES), jnp.float32),
        ]
        + [pltpu.VMEM(c.shape, c.dtype) for c in constants]
        + [
            pltpu.SemaphoreType.DMA((sends,)),
            pltpu.SemaphoreType.DMA((len(PARTS), count)),
            pltpu.SemaphoreType.DMA((2, max(spins - 1, 1))),
            pltpu.SemaphoreType.DMA((8,)),
        ],
        compiler_params=pltpu.CompilerParams(
            collective_id=0,
            has_side_effects=True,
            vmem_limit_bytes=60 * 1024 * 1024,
        ),
    )(orbitals.reshape(rows, LANES), potential.reshape(rows, LANES), *constants)
    updated = orbitals.reshape(rows, LANES) + step_length * negative
    return updated.reshape(orbitals.shape), (-negative).reshape(orbitals.shape)


def solution(mesh):
    return jax.shard_map(
        functools.partial(per_device, mesh.shape["band"], mesh.shape["spin"]),
        mesh=mesh,
        in_specs=(P("spin", "band", None), P()),
        out_specs=(P("spin", "band", None), P("spin", "band", None)),
        check_vma=False,
    )
```
